32 devices in a mesh: seq: 8 (over z, x), tp: 4 (over y, core).
Axes of the slice: x: 2, y: 2, z: 4, core: 2. Of those that a mesh axis runs over, the one named last changes fastest.
Arguments:
- hidden: bfloat16 [4096, 4096], P(('seq', 'tp')), may hold values from -640 to 640
- norm_gain: float32 [4096], replicated, may hold values from 0.5 to 1.5
- w_query: bfloat16 [4096, 2048], P(None, 'tp'), may hold values from -0.078125 to 0.078125
- w_key: bfloat16 [4096, 1024], P(None, 'tp'), may hold values from -2.421875 to 2.421875
- w_value: bfloat16 [4096, 1024], P(None, 'tp'), may hold values from -0.09375 to 0.09375
- doc_start: int32 [4096], P('seq'), may hold values from 0 to 4095, as said below
- block_owner: int32 [128], P('seq'), may hold values from 0 to 7, as said below
Outputs:
- context_rows: bfloat16 [4096, 2048], P(('seq', 'tp'))
- key_cache: bfloat16 [6144, 1024], P('seq', 'tp')
- value_cache: bfloat16 [6144, 1024], P('seq', 'tp')
The draws below stay inside these ranges and needn't reach their ends.
Inputs may be any that keep to these rules, and one draw needn't show every extreme that they name: `doc_start`: rows with equal values form one document: consecutive rows beginning at the row whose number is that value. Every document has at most 256 rows and one has exactly 256; all but the last have at least 64. `block_owner`: owner numbers never fall along the blocks. Owner o holds the blocks from o * 16 + e(o) up to (o + 1) * 16 + e(o + 1) - 1, where -4 <= e <= 4 and e is 0 at both ends of the axis; so an owner holds between 8 and 24 blocks, and some owner holds exactly 24.
All inputs are finite; a program needn't handle non-finite values.
Results may differ from the reference program's by a relative error of at most 0.0078.
Values may be sent and summed in bfloat16 or wider, within the bound.
A program may use at most 128 MiB of HBM per device.

```python
import jax
import jax.numpy as jnp
from jax import lax

D = 4096
KVH = 8
HD = 128
QH = 16
TOK_DEV = 512
BLK = 32
DOC_MIN = 64
DOC_MAX = 256
TOKENS = 4096
BPD = 16
SPILL = 4
CAP_BLK = 24
NBLK = 128
CACHE_ROWS = 6144
N_SEQ = 8


def draw_hidden(key, part):
    base_key = jax.random.fold_in(key, 101)
    row_key = jax.random.fold_in(key, 102)
    column_key = jax.random.fold_in(key, 103)
    row_scale = jnp.exp(jax.random.uniform(row_key, (TOKENS, 1), jnp.float32, 0.0, 2.3))
    column_scale = jnp.exp(jax.random.uniform(column_key, (1, D), jnp.float32, 0.0, 2.3))
    jitter = jnp.clip(jax.random.normal(base_key, (TOKENS, D), jnp.float32), -5.0, 5.0)
    values = jitter * row_scale * column_scale
    return values.astype(jnp.bfloat16)


def query_base(key):
    jitter = jax.random.normal(jax.random.fold_in(key, 201), (D, QH * HD), jnp.float32)
    return jnp.clip(jitter, -5.0, 5.0) * D ** (-0.5)


def draw_w_query(key, part):
    return query_base(key).astype(jnp.bfloat16)


def draw_w_key(key, part):
    jitter = jax.random.normal(jax.random.fold_in(key, 204), (D, KVH * HD), jnp.float32)
    values = jnp.clip(jitter, -5.0, 5.0) * D ** (-0.5)
    return values.astype(jnp.bfloat16)


def draw_doc_start(key, part):
    doc_count = TOKENS // DOC_MIN + 1
    lengths = jax.random.randint(jax.random.fold_in(key, 301), (doc_count,), DOC_MIN, DOC_MAX + 1)
    longest = jax.random.randint(jax.random.fold_in(key, 302), (), 1, TOKENS // DOC_MAX)
    lengths = jnp.where(jnp.arange(doc_count) == longest, DOC_MAX, lengths).astype(jnp.int32)
    last_home = TOKENS - TOK_DEV
    aligned = jnp.any(jnp.cumsum(lengths).astype(jnp.int32) == last_home)
    nudge = jnp.where(lengths[0] < DOC_MAX, 1, -1).astype(jnp.int32)
    lengths = lengths.at[0].add(jnp.where(aligned, nudge, 0).astype(jnp.int32))
    doc_ends = jnp.cumsum(lengths).astype(jnp.int32)
    doc_starts = doc_ends - lengths
    picked = jnp.searchsorted(doc_ends, jnp.arange(TOKENS, dtype=jnp.int32), side='right')
    return doc_starts[picked].astype(jnp.int32)


def draw_block_owner(key, part):
    owners = NBLK // BPD
    shifts = jax.random.randint(jax.random.fold_in(key, 401), (owners + 1,), -SPILL, SPILL + 1)
    marked = jax.random.randint(jax.random.fold_in(key, 402), (), 1, owners - 1)
    places = jnp.arange(owners + 1)
    shifts = jnp.where(places == marked, -SPILL, shifts)
    shifts = jnp.where(places == marked + 1, SPILL, shifts)
    shifts = jnp.where((places == 0) | (places == owners), 0, shifts)
    bounds = places * BPD + shifts
    blocks = jnp.arange(NBLK)
    interior = bounds[1:owners]
    return jnp.sum((blocks[:, None] >= interior[None, :]).astype(jnp.int32), axis=1).astype(jnp.int32)


def block_levels(key, shape, cuts, least, high):
    loudness, own = 1.0, jax.random.fold_in(key, 6)
    for axis_at, shards_of in cuts:
        heights = jnp.exp(jax.random.uniform(jax.random.fold_in(own, axis_at), (shards_of,), jnp.float32, least / len(cuts), high / len(cuts)))
        loudness = loudness * jnp.repeat(heights, shape[axis_at] // shards_of).reshape([-1 if axis == axis_at else 1 for axis in range(len(shape))])
    return loudness


def noise(stream_key, shape, width, bound, pieces=(), kind=jnp.bfloat16):
    entries = width * jax.random.normal(stream_key, shape, jnp.float32)
    if pieces:
        entries = entries * block_levels(stream_key, shape, pieces, -0.22, 0.18)
    return jnp.clip(entries, -bound, bound).astype(kind)


def setup_inputs(seed: int = 0) -> dict:
    splits = jax.random.split(jax.random.key(seed), 8)
    return {
        "hidden": draw_hidden(jax.random.fold_in(splits[7], 71), 0),
        "norm_gain": jnp.clip(1.0 + 0.1 * jax.random.normal(splits[1], (D,), jnp.float32), 0.5, 1.5),
        "w_query": draw_w_query(jax.random.fold_in(splits[7], 71), 0),
        "w_key": draw_w_key(jax.random.fold_in(splits[7], 71), 0),
        "w_value": noise(splits[4], (D, KVH * HD), D ** -0.5, 0.09375, ((1, 4),)),
        "doc_start": draw_doc_start(jax.random.fold_in(splits[7], 71), 0),
        "block_owner": draw_block_owner(jax.random.fold_in(splits[7], 71), 0),
    }


EPS = 1e-05
ROPE_BASE = 500000.0

def rotate(packed, positions, head_count):
    row_count = packed.shape[0]
    head_width = packed.shape[1] // head_count
    half_width = head_width // 2
    frequency = jnp.power(ROPE_BASE, -jnp.arange(half_width, dtype=jnp.float32) * (2.0 / head_width))
    angles = positions.astype(jnp.float32)[:, None] * frequency[None, :]
    cosine = jnp.cos(angles)[:, None, :]
    sine_part = jnp.sin(angles)[:, None, :]
    reshaped = packed.reshape(row_count, head_count, head_width)
    first_half = reshaped[:, :, :half_width]
    second = reshaped[:, :, half_width:]
    rotated = jnp.concatenate([first_half * cosine - second * sine_part, second * cosine + first_half * sine_part], axis=2)
    return rotated.reshape(row_count, head_count * head_width)

def project(rows_in, norm_gain, w_query, w_key, w_value, positions):
    widened = rows_in.astype(jnp.float32)
    inverse_rms = lax.rsqrt(lax.optimization_barrier(jnp.mean(widened * widened, axis=1, keepdims=True)) + EPS)
    normed = (widened * inverse_rms * norm_gain.astype(jnp.float32)[None, :]).astype(jnp.bfloat16)
    queries = jnp.dot(normed, w_query, preferred_element_type=jnp.float32)
    keys_f = jnp.dot(normed, w_key, preferred_element_type=jnp.float32)
    values_f = jnp.dot(normed, w_value, preferred_element_type=jnp.float32)
    queries = rotate(queries, positions, queries.shape[1] // HD).astype(jnp.bfloat16)
    keys_f = rotate(keys_f, positions, keys_f.shape[1] // HD).astype(jnp.bfloat16)
    return (queries, keys_f, values_f.astype(jnp.bfloat16))

def attend(queries, keys_in, values_in, query_doc, query_row, key_doc, key_row, key_live, offset):
    row_count = queries.shape[0]
    key_count = keys_in.shape[0]
    groups = keys_in.shape[1] // HD
    per_group = queries.shape[1] // keys_in.shape[1]
    query_four = queries.astype(jnp.float32).reshape(row_count, groups, per_group, HD)
    key_three = keys_in.astype(jnp.float32).reshape(key_count, groups, HD)
    value_three = values_in.astype(jnp.float32).reshape(key_count, groups, HD)
    scores = jnp.einsum('rgjd,kgd->gjrk', query_four, key_three) * HD ** (-0.5)
    allowed = (query_doc[:, None] == key_doc[None, :]) & (key_row[None, :] <= query_row[:, None]) & (key_live[None, :] > 0)
    allowed = allowed | (jnp.arange(key_count)[None, :] == jnp.arange(row_count)[:, None] + offset)
    scores = jnp.where(allowed[None, None], scores, -jnp.inf)
    highest = lax.optimization_barrier(jnp.max(scores, axis=3, keepdims=True))
    weights = jnp.exp(scores - highest)
    weights = (weights / lax.optimization_barrier(jnp.sum(weights, axis=3, keepdims=True))).astype(jnp.bfloat16)
    blended = jnp.einsum('gjrk,kgd->rgjd', weights.astype(jnp.float32), value_three)
    return blended.astype(jnp.bfloat16).reshape(row_count, groups * per_group * HD)

def reference(hidden, norm_gain, w_query, w_key, w_value, doc_start, block_owner):
    row_number = jnp.arange(TOKENS, dtype=jnp.int32)
    queries, keys_bf, values_bf = project(hidden, norm_gain, w_query, w_key, w_value, row_number - doc_start)
    kv_width = keys_bf.shape[1]
    padded_keys = jnp.concatenate([jnp.zeros((TOK_DEV, kv_width), jnp.bfloat16), keys_bf], axis=0)
    padded_values = jnp.concatenate([jnp.zeros((TOK_DEV, kv_width), jnp.bfloat16), values_bf], axis=0)
    padded_doc = jnp.concatenate([jnp.full((TOK_DEV,), -1, jnp.int32), doc_start.astype(jnp.int32)], axis=0)
    padded_row = jnp.concatenate([jnp.arange(TOK_DEV, dtype=jnp.int32) - TOK_DEV, row_number], axis=0)

    def one_block(index):
        start = (index * TOK_DEV).astype(jnp.int32)
        block_queries = lax.dynamic_slice_in_dim(queries, start, TOK_DEV, 0)
        block_doc = lax.dynamic_slice_in_dim(doc_start.astype(jnp.int32), start, TOK_DEV, 0)
        block_row = lax.dynamic_slice_in_dim(row_number, start, TOK_DEV, 0)
        near_keys = lax.dynamic_slice_in_dim(padded_keys, start, 2 * TOK_DEV, 0)
        near_values = lax.dynamic_slice_in_dim(padded_values, start, 2 * TOK_DEV, 0)
        near_doc = lax.dynamic_slice_in_dim(padded_doc, start, 2 * TOK_DEV, 0)
        near_row = lax.dynamic_slice_in_dim(padded_row, start, 2 * TOK_DEV, 0)
        near_live = (near_doc >= 0).astype(jnp.int32)
        return attend(block_queries, near_keys, near_values, block_doc, block_row, near_doc, near_row, near_live, TOK_DEV)
    context_rows = lax.map(one_block, jnp.arange(N_SEQ, dtype=jnp.int32)).reshape(TOKENS, queries.shape[1])
    owners = jnp.arange(N_SEQ, dtype=jnp.int32)
    frame_block = owners[:, None] * BPD - SPILL + jnp.arange(CAP_BLK, dtype=jnp.int32)[None, :]
    inside = (frame_block >= 0) & (frame_block < NBLK)
    clamped = jnp.clip(frame_block, 0, NBLK - 1)
    owned = inside & (block_owner.astype(jnp.int32)[clamped] == owners[:, None])
    key_blocks = keys_bf.reshape(NBLK, BLK, kv_width)
    value_blocks = values_bf.reshape(NBLK, BLK, kv_width)
    key_cache = jnp.where(owned[:, :, None, None], key_blocks[clamped], jnp.zeros((), jnp.bfloat16)).reshape(CACHE_ROWS, kv_width)
    value_cache = jnp.where(owned[:, :, None, None], value_blocks[clamped], jnp.zeros((), jnp.bfloat16)).reshape(CACHE_ROWS, kv_width)
    return (context_rows, key_cache, value_cache)
```

```python
import functools

import jax
import jax.numpy as jnp
import numpy as np
from jax import lax
from jax.experimental import pallas as pl
from jax.experimental.pallas import tpu as pltpu
from jax.sharding import PartitionSpec as P

HD = 128
DOC_MAX = 256
EPS = 1e-05
ROPE_BASE = 500000.0
HALVES = 2
COLS = 4
F32 = jnp.float32
BF16 = jnp.bfloat16
MESH = pl.DeviceIdType.MESH


def kernel(
    n_seq, block_rows,
    x_hbm, gain, wq_hbm, wk_hbm, wv_hbm, doc, owner, freq,
    ctx_out, kc_out, vc_out,
    xin, hid, w, acc, acc2, cosb, sinb, docb, qb, kb, vb, ob, ctxb, kst, vst,
    loc, sib_s, sib_r, far_s, far_r, fwd_s, fwd_r,
    rt_s, rt_r, lf_s, lf_r, own_s, own_r, ctx_s, ctx_r,
):
    me = lax.axis_index("tp")
    seq = lax.axis_index("seq")
    rows, width = xin.shape
    tp = hid.shape[0]
    home = rows * tp
    reach = DOC_MAX
    spill = kc_out.shape[0] // 2 - home // 2
    half = rows // HALVES
    cw = width // COLS
    kw = kb.shape[1]
    qw = qb.shape[1]
    nw = w.shape[0]
    peer = [me, me + 1 - 2 * (me % 2), (me + 2) % 4, 3 - me]
    has_left = seq > 0
    has_right = seq < n_seq - 1
    upper = me >= 2

    cx = pltpu.make_async_copy(x_hbm, xin, loc.at[0])
    cx.start()
    wcopies = []
    for n in range(nw):
        if n < qw // kw:
            src = wq_hbm.at[:, n * kw:(n + 1) * kw]
        elif n == nw - 2:
            src = wk_hbm
        else:
            src = wv_hbm
        c = pltpu.make_async_copy(src, w.at[n], loc.at[1 + n])
        c.start()
        wcopies.append(c)

    barrier = pltpu.get_barrier_semaphore()
    for s in (1, 2, 3):
        pl.semaphore_signal(barrier, inc=1, device_id={"tp": peer[s]}, device_id_type=MESH)

    @pl.when(has_left)
    def _():
        pl.semaphore_signal(barrier, inc=1, device_id={"seq": seq - 1}, device_id_type=MESH)

    @pl.when(has_right)
    def _():
        pl.semaphore_signal(barrier, inc=1, device_id={"seq": seq + 1}, device_id_type=MESH)

    cx.wait()

    def norm_rows(i, carry):
        at = pl.ds(pl.multiple_of(i * 16, 16), 16)
        wide = xin[at, :].astype(F32)
        inv = lax.rsqrt(jnp.mean(wide * wide, axis=1, keepdims=True) + EPS)
        hid[0, at, :] = (wide * inv * gain[...]).astype(BF16)
        return carry

    lax.fori_loop(0, rows // 16, norm_rows, 0)

    pl.semaphore_wait(barrier, 3 + has_left.astype(jnp.int32) + has_right.astype(jnp.int32))

    def part(slot, c):
        h, k = c // COLS, c % COLS
        return hid.at[slot, pl.ds(h * half, half), pl.ds(k * cw, cw)]

    def far_copy(c):
        return pltpu.make_async_remote_copy(
            src_ref=part(0, c), dst_ref=part(2, c), send_sem=far_s.at[c], recv_sem=far_r.at[c],
            device_id={"tp": peer[2]}, device_id_type=MESH)

    def fwd_copy(c):
        return pltpu.make_async_remote_copy(
            src_ref=part(2, c), dst_ref=part(3, c), send_sem=fwd_s.at[c], recv_sem=fwd_r.at[c],
            device_id={"tp": peer[1]}, device_id_type=MESH)

    sib = pltpu.make_async_remote_copy(
        src_ref=hid.at[0], dst_ref=hid.at[1], send_sem=sib_s.at[0], recv_sem=sib_r.at[0],
        device_id={"tp": peer[1]}, device_id_type=MESH)
    chunks = HALVES * COLS
    for c in range(chunks):
        far_copy(c).start()
    sib.start()

    def own_copy(d):
        return pltpu.make_async_remote_copy(
            src_ref=owner, dst_ref=ob.at[d], send_sem=own_s.at[d], recv_sem=own_r.at[d],
            device_id={"seq": seq + 1 if d == 0 else seq - 1}, device_id_type=MESH)

    kv = (kb, vb)

    def right_copy(t, b, h):
        u = (t * 2 + b) * HALVES + h
        lo = b * rows + h * half
        return pltpu.make_async_remote_copy(
            src_ref=kv[t].at[pl.ds(home + lo, half)], dst_ref=kv[t].at[pl.ds(lo, half)],
            send_sem=rt_s.at[u], recv_sem=rt_r.at[u],
            device_id={"seq": seq + 1}, device_id_type=MESH)

    def left_copy(t, h):
        u = t * HALVES + h
        return pltpu.make_async_remote_copy(
            src_ref=kv[t].at[pl.ds(reach + h * half, half)],
            dst_ref=kv[t].at[pl.ds(reach + home + h * half, half)],
            send_sem=lf_s.at[u], recv_sem=lf_r.at[u],
            device_id={"seq": seq - 1}, device_id_type=MESH)

    rights = [(t, b, h) for h in range(HALVES) for t in range(2) for b in range(2)]
    lefts = [(t, h) for h in range(HALVES) for t in range(2)]

    @pl.when(has_right)
    def _():
        own_copy(0).start()

    @pl.when(has_left)
    def _():
        own_copy(1).start()

    @pl.when(jnp.logical_not(has_left))
    def _():
        kb[pl.ds(0, reach), :] = jnp.zeros((reach, kw), BF16)
        vb[pl.ds(0, reach), :] = jnp.zeros((reach, kw), BF16)
        ob[0] = jnp.full(owner.shape, -1, jnp.int32)

    @pl.when(jnp.logical_not(has_right))
    def _():
        kb[pl.ds(reach + home, spill), :] = jnp.zeros((spill, kw), BF16)
        vb[pl.ds(reach + home, spill), :] = jnp.zeros((spill, kw), BF16)
        ob[1] = jnp.full(owner.shape, -1, jnp.int32)

    row_i = lax.broadcasted_iota(jnp.int32, (rows, rows), 0)
    col_i = lax.broadcasted_iota(jnp.int32, (rows, rows), 1)
    first = (seq * home).astype(F32)
    for j in range(tp):
        line = jnp.broadcast_to(doc[j:j + 1, :].astype(F32) - first, (rows, rows))
        column = jnp.sum(jnp.where(row_i == col_i, line, 0.0), axis=1, keepdims=True)
        start = jnp.broadcast_to(column, (rows, rows))
        docb[j * rows:(j + 1) * rows, :] = start
        angle = (row_i.astype(F32) + float(j * rows) - start) * freq[...]
        cosb[j * rows:(j + 1) * rows, :] = jnp.cos(angle)
        sine = jnp.sin(angle)
        sinb[j * rows:(j + 1) * rows, :] = jnp.where(col_i < HD // 2, -sine, sine)

    def finish(ref, src_row, count, at):
        cos = cosb[pl.ds(at, count), :]
        sin = sinb[pl.ds(at, count), :]

        def turned(n, e):
            y = ref[n, src_row:src_row + count, e * HD:(e + 1) * HD]
            return (y * cos + pltpu.roll(y, HD // 2, 1) * sin).astype(BF16)

        for n in range(nw - 2):
            for e in range(kw // HD):
                lane = n * kw + e * HD
                qb[pl.ds(at, count), lane:lane + HD] = turned(n, e)
        put = pl.ds(at + reach, count)
        for e in range(kw // HD):
            kb[put, e * HD:(e + 1) * HD] = turned(nw - 2, e)
        vb[put, :] = ref[nw - 1, src_row:src_row + count, :].astype(BF16)

    for c in wcopies:
        c.wait()
    sib.wait_recv()

    def early(n, carry):
        lhs = hid[0:2].reshape(2 * rows, width)
        acc[n] = jnp.dot(lhs, w[n], preferred_element_type=F32)
        return carry

    lax.fori_loop(0, nw, early, 0)
    for s in range(2):
        finish(acc, s * rows, rows, pl.multiple_of(peer[s] * rows, rows))

    @pl.when(jnp.logical_and(upper, has_right))
    def _():
        for u in rights:
            right_copy(*u).start()

    @pl.when(jnp.logical_and(jnp.logical_not(upper), has_left))
    def _():
        for u in lefts:
            left_copy(*u).start()

    for h in range(HALVES):
        for k in range(COLS):
            c = h * COLS + k
            far_copy(c).wait_recv()
            fwd_copy(c).start()
            fwd_copy(c).wait_recv()

            def late(n, carry):
                lhs = hid[2:4, h * half:(h + 1) * half, k * cw:(k + 1) * cw].reshape(2 * half, cw)
                got = jnp.dot(lhs, w[n, k * cw:(k + 1) * cw, :], preferred_element_type=F32)
                if k == 0:
                    acc2[n] = got
                else:
                    acc2[n] += got
                return carry

            lax.fori_loop(0, nw, late, 0)
        for s in range(2):
            finish(acc2, s * half, half, pl.multiple_of(peer[2 + s] * rows + h * half, half))

        @pl.when(jnp.logical_and(jnp.logical_not(upper), has_right))
        def _():
            for u in rights:
                if u[-1] == h:
                    right_copy(*u).start()

        @pl.when(jnp.logical_and(upper, has_left))
        def _():
            for u in lefts:
                if u[-1] == h:
                    left_copy(*u).start()

    def wait_left():
        for u in rights:
            right_copy(*u).wait_recv()

    @pl.when(jnp.logical_and(upper, has_left))
    def _():
        wait_left()

    window = rows + reach
    groups = kw // HD
    per = qw // kw
    ci = lax.broadcasted_iota(jnp.int32, (rows, window), 1)
    ri = lax.broadcasted_iota(jnp.int32, (rows, window), 0)

    def attend(j):
        base = pl.multiple_of(j * rows, rows)
        start = docb[pl.ds(base, rows), :]
        start = jnp.concatenate([start] * (window // rows), axis=1)
        local = ci + (j * rows - reach)
        allowed = jnp.logical_and(local.astype(F32) >= start, ci <= ri + reach)
        allowed = jnp.concatenate([allowed] * per, axis=0)
        for g in range(groups):
            q = jnp.concatenate(
                [qb[pl.ds(base, rows), (g * per + e) * HD:(g * per + e + 1) * HD] for e in range(per)], axis=0)
            keys = kb[pl.ds(base, window), g * HD:(g + 1) * HD]
            vals = vb[pl.ds(base, window), g * HD:(g + 1) * HD]
            sc = lax.dot_general(q, keys, (((1,), (1,)), ((), ())), preferred_element_type=F32) * HD ** (-0.5)
            sc = jnp.where(allowed, sc, -jnp.inf)
            ex = jnp.exp(sc - jnp.max(sc, axis=1, keepdims=True))
            wt = (ex * (1.0 / jnp.sum(ex, axis=1, keepdims=True))).astype(BF16)
            o = jnp.dot(wt, vals, preferred_element_type=F32).astype(BF16)
            for e in range(per):
                ctxb[j, :, (g * per + e) * HD:(g * per + e + 1) * HD] = o[e * rows:(e + 1) * rows]

    def ctx_copy(s):
        return pltpu.make_async_remote_copy(
            src_ref=ctxb.at[peer[s]], dst_ref=ctx_out.at[:, pl.ds(pl.multiple_of(me * qw, qw), qw)],
            send_sem=ctx_s.at[s], recv_sem=ctx_r.at[s],
            device_id={"tp": peer[s]}, device_id_type=MESH)

    for s in (2, 3):
        attend(peer[s])
        ctx_copy(s).start()

    @pl.when(has_right)
    def _():
        own_copy(1).wait_recv()
        for u in lefts:
            left_copy(*u).wait_recv()

    @pl.when(has_left)
    def _():
        own_copy(0).wait_recv()

    side = spill // block_rows
    blocks = home // block_rows

    def cache(b):
        if b < side:
            line = ob[0, blocks - side + b:blocks - side + b + 1, :]
        elif b < side + blocks:
            line = owner[b - side:b - side + 1, :]
        else:
            line = ob[1, b - side - blocks:b - side - blocks + 1, :]
        line = jnp.broadcast_to(jnp.where(line == seq, 1.0, 0.0), (block_rows, HD))
        live = jnp.concatenate([line] * (kw // HD), axis=1) > 0.5
        to = slice(b * block_rows, (b + 1) * block_rows)
        at = slice(reach - spill + b * block_rows, reach - spill + (b + 1) * block_rows)
        kst[to, :] = jnp.where(live, kb[at, :].astype(F32), 0.0).astype(BF16)
        vst[to, :] = jnp.where(live, vb[at, :].astype(F32), 0.0).astype(BF16)

    for b in range(side, 2 * side + blocks):
        cache(b)

    @pl.when(jnp.logical_and(jnp.logical_not(upper), has_left))
    def _():
        wait_left()

    attend(peer[1])
    ctx_copy(1).start()
    attend(peer[0])
    mine = pltpu.make_async_copy(
        ctxb.at[me], ctx_out.at[:, pl.ds(pl.multiple_of(me * qw, qw), qw)], loc.at[0])
    mine.start()
    for b in range(side):
        cache(b)
    ck = pltpu.make_async_copy(kst, kc_out, loc.at[1])
    cv = pltpu.make_async_copy(vst, vc_out, loc.at[2])
    ck.start()
    cv.start()

    sib.wait_send()
    for c in range(chunks):
        far_copy(c).wait_send()
        fwd_copy(c).wait_send()

    @pl.when(has_right)
    def _():
        own_copy(0).wait_send()
        for u in rights:
            right_copy(*u).wait_send()

    @pl.when(has_left)
    def _():
        own_copy(1).wait_send()
        for u in lefts:
            left_copy(*u).wait_send()

    mine.wait()
    ck.wait()
    cv.wait()
    for s in (1, 2, 3):
        ctx_copy(s).wait_send()
        pltpu.make_async_remote_copy(
            src_ref=ctxb.at[peer[s]],
            dst_ref=ctx_out.at[:, pl.ds(pl.multiple_of(peer[s] * qw, qw), qw)],
            send_sem=ctx_s.at[s], recv_sem=ctx_r.at[s],
            device_id={"tp": peer[s]}, device_id_type=MESH).wait_recv()


def shards(n_seq, tp, hidden, norm_gain, w_query, w_key, w_value, doc_start, block_owner):
    rows, width = hidden.shape
    home = doc_start.shape[0]
    qw, kw = w_query.shape[1], w_key.shape[1]
    home_blocks = block_owner.shape[0]
    block_rows = home // home_blocks
    spill = home_blocks // 4 * block_rows
    frame = home + 2 * spill
    assert tp == 4 and spill == rows and DOC_MAX == 2 * rows and rows == HD
    lane = np.arange(HD) % (HD // 2)
    freq = jnp.asarray((ROPE_BASE ** (-2.0 * lane / HD)).astype(np.float32)[None, :])
    nw = qw // kw + 2
    ctx, kc, vc = pl.pallas_call(
        functools.partial(kernel, n_seq, block_rows),
        out_shape=(
            jax.ShapeDtypeStruct((rows, qw * tp), BF16),
            jax.ShapeDtypeStruct((frame, kw), BF16),
            jax.ShapeDtypeStruct((frame, kw), BF16),
        ),
        in_specs=[
            pl.BlockSpec(memory_space=pl.ANY),
            pl.BlockSpec(memory_space=pltpu.VMEM),
            pl.BlockSpec(memory_space=pl.ANY),
            pl.BlockSpec(memory_space=pl.ANY),
            pl.BlockSpec(memory_space=pl.ANY),
            pl.BlockSpec(memory_space=pltpu.VMEM),
            pl.BlockSpec(memory_space=pltpu.VMEM),
            pl.BlockSpec(memory_space=pltpu.VMEM),
        ],
        out_specs=[pl.BlockSpec(memory_space=pl.ANY)] * 3,
        scratch_shapes=[
            pltpu.VMEM((rows, width), BF16),
            pltpu.VMEM((tp, rows, width), BF16),
            pltpu.VMEM((nw, width, kw), BF16),
            pltpu.VMEM((nw, 2 * rows, kw), F32),
            pltpu.VMEM((nw, 2 * rows // HALVES, kw), F32),
            pltpu.VMEM((home, HD), F32),
            pltpu.VMEM((home, HD), F32),
            pltpu.VMEM((home, HD), F32),
            pltpu.VMEM((home, qw), BF16),
            pltpu.VMEM((DOC_MAX + home + spill, kw), BF16),
            pltpu.VMEM((DOC_MAX + home + spill, kw), BF16),
            pltpu.VMEM((2, home_blocks, HD), jnp.int32),
            pltpu.VMEM((tp, rows, qw), BF16),
            pltpu.VMEM((frame, kw), BF16),
            pltpu.VMEM((frame, kw), BF16),
            pltpu.SemaphoreType.DMA((1 + nw,)),
            pltpu.SemaphoreType.DMA((1,)),
            pltpu.SemaphoreType.DMA((1,)),
            pltpu.SemaphoreType.DMA((HALVES * COLS,)),
            pltpu.SemaphoreType.DMA((HALVES * COLS,)),
            pltpu.SemaphoreType.DMA((HALVES * COLS,)),
            pltpu.SemaphoreType.DMA((HALVES * COLS,)),
            pltpu.SemaphoreType.DMA((4 * HALVES,)),
            pltpu.SemaphoreType.DMA((4 * HALVES,)),
            pltpu.SemaphoreType.DMA((2 * HALVES,)),
            pltpu.SemaphoreType.DMA((2 * HALVES,)),
            pltpu.SemaphoreType.DMA((2,)),
            pltpu.SemaphoreType.DMA((2,)),
            pltpu.SemaphoreType.DMA((4,)),
            pltpu.SemaphoreType.DMA((4,)),
        ],
        compiler_params=pltpu.CompilerParams(
            collective_id=0, has_side_effects=True, vmem_limit_bytes=48 * 1024 * 1024),
    )(
        hidden, norm_gain.reshape(1, width), w_query, w_key, w_value,
        doc_start.reshape(tp, rows),
        jnp.broadcast_to(block_owner[:, None], (home_blocks, HD)), freq,
    )
    return ctx, kc, vc


def solution(mesh):
    return jax.shard_map(
        functools.partial(shards, mesh.shape["seq"], mesh.shape["tp"]),
        mesh=mesh,
        in_specs=(
            P(("seq", "tp"), None), P(), P(None, "tp"), P(None, "tp"), P(None, "tp"),
            P("seq"), P("seq"),
        ),
        out_specs=(P(("seq", "tp"), None), P("seq", "tp"), P("seq", "tp")),
        check_vma=False,
    )
```

```python
import functools

import jax
import jax.numpy as jnp
import numpy as np
from jax import lax
from jax.experimental import pallas as pl
from jax.experimental.pallas import tpu as pltpu
from jax.sharding import PartitionSpec as P

HD = 128
DOC_MAX = 256
EPS = 1e-05
ROPE_BASE = 500000.0
HALVES = 2
COLS = 4
F32 = jnp.float32
BF16 = jnp.bfloat16
MESH = pl.DeviceIdType.MESH


def kernel(
    n_seq, block_rows,
    x_hbm, gain_hbm, wq_hbm, wk_hbm, wv_hbm, doc_hbm, owner_hbm, freq_hbm,
    ctx_out, kc_out, vc_out,
    gain, doc, owner, freq, ownb, xin, hid, w, acc, acc2, cosb, sinb, docb, qb, kb, vb, ob, ctxb, kst, vst,
    loc, sib_s, sib_r, far_s, far_r, fwd_s, fwd_r,
    rt_s, rt_r, lf_s, lf_r, own_s, own_r, ctx_s, ctx_r,
):
    me = lax.axis_index("tp")
    seq = lax.axis_index("seq")
    rows, width = xin.shape
    tp = hid.shape[0]
    home = rows * tp
    reach = DOC_MAX
    spill = kc_out.shape[0] // 2 - home // 2
    half = rows // HALVES
    cw = width // COLS
    kw = kb.shape[1]
    qw = qb.shape[1]
    nw = w.shape[0]
    peer = [me, me + 1 - 2 * (me % 2), (me + 2) % 4, 3 - me]
    has_left = seq > 0
    has_right = seq < n_seq - 1
    upper = me >= 2

    cx = pltpu.make_async_copy(x_hbm, xin, loc.at[0])
    cx.start()
    small = [
        pltpu.make_async_copy(a, b, loc.at[1 + nw + i])
        for i, (a, b) in enumerate(
            ((gain_hbm, gain), (doc_hbm, doc), (owner_hbm, owner), (freq_hbm, freq)))
    ]
    for c in small:
        c.start()
    wcopies = []
    for n in range(nw):
        if n < qw // kw:
            src = wq_hbm.at[:, n * kw:(n + 1) * kw]
        elif n == nw - 2:
            src = wk_hbm
        else:
            src = wv_hbm
        c = pltpu.make_async_copy(src, w.at[n], loc.at[1 + n])
        c.start()
        wcopies.append(c)

    barrier = pltpu.get_barrier_semaphore()
    for s in (1, 2, 3):
        pl.semaphore_signal(barrier, inc=1, device_id={"tp": peer[s]}, device_id_type=MESH)

    @pl.when(has_left)
    def _():
        pl.semaphore_signal(barrier, inc=1, device_id={"seq": seq - 1}, device_id_type=MESH)

    @pl.when(has_right)
    def _():
        pl.semaphore_signal(barrier, inc=1, device_id={"seq": seq + 1}, device_id_type=MESH)

    cx.wait()
    for c in small:
        c.wait()

    def norm_rows(i, carry):
        at = pl.ds(pl.multiple_of(i * 16, 16), 16)
        wide = xin[at, :].astype(F32)
        inv = lax.rsqrt(jnp.mean(wide * wide, axis=1, keepdims=True) + EPS)
        hid[0, at, :] = (wide * inv * gain[...]).astype(BF16)
        return carry

    lax.fori_loop(0, rows // 16, norm_rows, 0)

    pl.semaphore_wait(barrier, 3 + has_left.astype(jnp.int32) + has_right.astype(jnp.int32))

    def part(slot, c):
        h, k = c // COLS, c % COLS
        return hid.at[slot, pl.ds(h * half, half), pl.ds(k * cw, cw)]

    def far_copy(c):
        return pltpu.make_async_remote_copy(
            src_ref=part(0, c), dst_ref=part(2, c), send_sem=far_s.at[c], recv_sem=far_r.at[c],
            device_id={"tp": peer[2]}, device_id_type=MESH)

    def fwd_copy(c):
        return pltpu.make_async_remote_copy(
            src_ref=part(2, c), dst_ref=part(3, c), send_sem=fwd_s.at[c], recv_sem=fwd_r.at[c],
            device_id={"tp": peer[1]}, device_id_type=MESH)

    sib = pltpu.make_async_remote_copy(
        src_ref=hid.at[0], dst_ref=hid.at[1], send_sem=sib_s.at[0], recv_sem=sib_r.at[0],
        device_id={"tp": peer[1]}, device_id_type=MESH)
    chunks = HALVES * COLS
    for c in range(chunks):
        far_copy(c).start()
    sib.start()

    def own_copy(d):
        return pltpu.make_async_remote_copy(
            src_ref=owner, dst_ref=ob.at[d], send_sem=own_s.at[d], recv_sem=own_r.at[d],
            device_id={"seq": seq + 1 if d == 0 else seq - 1}, device_id_type=MESH)

    kv = (kb, vb)

    def right_copy(t, b, h):
        u = (t * 2 + b) * HALVES + h
        lo = b * rows + h * half
        return pltpu.make_async_remote_copy(
            src_ref=kv[t].at[pl.ds(home + lo, half)], dst_ref=kv[t].at[pl.ds(lo, half)],
            send_sem=rt_s.at[u], recv_sem=rt_r.at[u],
            device_id={"seq": seq + 1}, device_id_type=MESH)

    def left_copy(t, h):
        u = t * HALVES + h
        return pltpu.make_async_remote_copy(
            src_ref=kv[t].at[pl.ds(reach + h * half, half)],
            dst_ref=kv[t].at[pl.ds(reach + home + h * half, half)],
            send_sem=lf_s.at[u], recv_sem=lf_r.at[u],
            device_id={"seq": seq - 1}, device_id_type=MESH)

    rights = [(t, b, h) for h in range(HALVES) for t in range(2) for b in range(2)]
    lefts = [(t, h) for h in range(HALVES) for t in range(2)]

    @pl.when(has_right)
    def _():
        own_copy(0).start()

    @pl.when(has_left)
    def _():
        own_copy(1).start()

    @pl.when(jnp.logical_not(has_left))
    def _():
        kb[pl.ds(0, reach), :] = jnp.zeros((reach, kw), BF16)
        vb[pl.ds(0, reach), :] = jnp.zeros((reach, kw), BF16)
        ob[0] = jnp.full(owner.shape, -1, jnp.int32)

    @pl.when(jnp.logical_not(has_right))
    def _():
        kb[pl.ds(reach + home, spill), :] = jnp.zeros((spill, kw), BF16)
        vb[pl.ds(reach + home, spill), :] = jnp.zeros((spill, kw), BF16)
        ob[1] = jnp.full(owner.shape, -1, jnp.int32)

    row_i = lax.broadcasted_iota(jnp.int32, (rows, rows), 0)
    col_i = lax.broadcasted_iota(jnp.int32, (rows, rows), 1)
    first = (seq * home).astype(F32)
    for j in range(tp):
        line = jnp.broadcast_to(doc[j:j + 1, :].astype(F32) - first, (rows, rows))
        column = jnp.sum(jnp.where(row_i == col_i, line, 0.0), axis=1, keepdims=True)
        start = jnp.broadcast_to(column, (rows, rows))
        docb[j * rows:(j + 1) * rows, :] = start
        angle = (row_i.astype(F32) + float(j * rows) - start) * freq[...]
        cosb[j * rows:(j + 1) * rows, :] = jnp.cos(angle)
        sine = jnp.sin(angle)
        sinb[j * rows:(j + 1) * rows, :] = jnp.where(col_i < HD // 2, -sine, sine)

    def turned(ref, n, e, src_row, count, at):
        y = ref[n, src_row:src_row + count, e * HD:(e + 1) * HD]
        cos = cosb[pl.ds(at, count), :]
        sin = sinb[pl.ds(at, count), :]
        return (y * cos + pltpu.roll(y, HD // 2, 1) * sin).astype(BF16)

    def finish_kv(ref, src_row, count, at):
        put = pl.ds(at + reach, count)
        for e in range(kw // HD):
            kb[put, e * HD:(e + 1) * HD] = turned(ref, nw - 2, e, src_row, count, at)
        vb[put, :] = ref[nw - 1, src_row:src_row + count, :].astype(BF16)

    def finish_q(ref, src_row, count, at):
        for n in range(nw - 2):
            for e in range(kw // HD):
                lane = n * kw + e * HD
                qb[pl.ds(at, count), lane:lane + HD] = turned(ref, n, e, src_row, count, at)

    for c in wcopies:
        c.wait()
    sib.wait_recv()

    def early(n, carry):
        lhs = hid[0:2].reshape(2 * rows, width)
        acc[n] = jnp.dot(lhs, w[n], preferred_element_type=F32)
        return carry

    def place(s, h=0):
        return pl.multiple_of(peer[s] * rows + h * half, half)

    lax.fori_loop(nw - 2, nw, early, 0)
    for s in range(2):
        finish_kv(acc, s * rows, rows, place(s))

    @pl.when(jnp.logical_and(upper, has_right))
    def _():
        for u in rights:
            right_copy(*u).start()

    @pl.when(jnp.logical_and(jnp.logical_not(upper), has_left))
    def _():
        for u in lefts:
            left_copy(*u).start()

    lax.fori_loop(0, nw - 2, early, 0)
    for s in range(2):
        finish_q(acc, s * rows, rows, place(s))

    for h in range(HALVES):
        for k in range(COLS):
            c = h * COLS + k
            far_copy(c).wait_recv()
            fwd_copy(c).start()
            fwd_copy(c).wait_recv()

            def late(n, carry):
                lhs = hid[2:4, h * half:(h + 1) * half, k * cw:(k + 1) * cw].reshape(2 * half, cw)
                got = jnp.dot(lhs, w[n, k * cw:(k + 1) * cw, :], preferred_element_type=F32)
                if k == 0:
                    acc2[n] = got
                else:
                    acc2[n] += got
                return carry

            lax.fori_loop(nw - 2, nw, late, 0)
            if k == COLS - 1:
                for s in range(2):
                    finish_kv(acc2, s * half, half, place(2 + s, h))

                @pl.when(jnp.logical_and(jnp.logical_not(upper), has_right))
                def _():
                    for u in rights:
                        if u[-1] == h:
                            right_copy(*u).start()

                @pl.when(jnp.logical_and(upper, has_left))
                def _():
                    for u in lefts:
                        if u[-1] == h:
                            left_copy(*u).start()

            lax.fori_loop(0, nw - 2, late, 0)
        for s in range(2):
            finish_q(acc2, s * half, half, place(2 + s, h))

    def wait_left():
        for u in rights:
            right_copy(*u).wait_recv()

    @pl.when(jnp.logical_and(upper, has_left))
    def _():
        wait_left()

    window = rows + reach
    groups = kw // HD
    per = qw // kw
    ci = lax.broadcasted_iota(jnp.int32, (rows, window), 1)
    ri = lax.broadcasted_iota(jnp.int32, (rows, window), 0)

    def attend(j):
        base = pl.multiple_of(j * rows, rows)
        start = docb[pl.ds(base, rows), :]
        start = jnp.concatenate([start] * (window // rows), axis=1)
        local = ci + (j * rows - reach)
        allowed = jnp.logical_and(local.astype(F32) >= start, ci <= ri + reach)
        allowed = jnp.concatenate([allowed] * per, axis=0)
        for g in range(groups):
            q = jnp.concatenate(
                [qb[pl.ds(base, rows), (g * per + e) * HD:(g * per + e + 1) * HD] for e in range(per)], axis=0)
            keys = kb[pl.ds(base, window), g * HD:(g + 1) * HD]
            vals = vb[pl.ds(base, window), g * HD:(g + 1) * HD]
            sc = lax.dot_general(q, keys, (((1,), (1,)), ((), ())), preferred_element_type=F32) * HD ** (-0.5)
            sc = jnp.where(allowed, sc, -jnp.inf)
            ex = jnp.exp(sc - jnp.max(sc, axis=1, keepdims=True))
            wt = (ex * (1.0 / jnp.sum(ex, axis=1, keepdims=True))).astype(BF16)
            o = jnp.dot(wt, vals, preferred_element_type=F32).astype(BF16)
            for e in range(per):
                ctxb[j, :, (g * per + e) * HD:(g * per + e + 1) * HD] = o[e * rows:(e + 1) * rows]

    def ctx_copy(s):
        return pltpu.make_async_remote_copy(
            src_ref=ctxb.at[peer[s]], dst_ref=ctx_out.at[:, pl.ds(pl.multiple_of(me * qw, qw), qw)],
            send_sem=ctx_s.at[s], recv_sem=ctx_r.at[s],
            device_id={"tp": peer[s]}, device_id_type=MESH)

    for s in (2, 3):
        attend(peer[s])
        ctx_copy(s).start()

    @pl.when(has_right)
    def _():
        own_copy(1).wait_recv()
        for u in lefts:
            left_copy(*u).wait_recv()

    @pl.when(has_left)
    def _():
        own_copy(0).wait_recv()

    side = spill // block_rows
    blocks = home // block_rows
    eye = (lax.broadcasted_iota(jnp.int32, (blocks, blocks), 0)
           == lax.broadcasted_iota(jnp.int32, (blocks, blocks), 1))
    for i in range(3):
        line = owner[...] if i == 1 else ob[i // 2]
        line = jnp.broadcast_to(line.astype(F32), (blocks, blocks))
        column = jnp.sum(jnp.where(eye, line, 0.0), axis=1, keepdims=True)
        ownb[i] = jnp.broadcast_to(column, (blocks, HD))
    seq_f = seq.astype(F32)

    def cache(b):
        if b < side:
            line = ownb[0, blocks - side + b:blocks - side + b + 1, :]
        elif b < side + blocks:
            line = ownb[1, b - side:b - side + 1, :]
        else:
            line = ownb[2, b - side - blocks:b - side - blocks + 1, :]
        line = jnp.broadcast_to(jnp.where(line == seq_f, 1.0, 0.0), (block_rows, HD))
        live = jnp.concatenate([line] * (kw // HD), axis=1) > 0.5
        to = slice(b * block_rows, (b + 1) * block_rows)
        at = slice(reach - spill + b * block_rows, reach - spill + (b + 1) * block_rows)
        kst[to, :] = jnp.where(live, kb[at, :].astype(F32), 0.0).astype(BF16)
        vst[to, :] = jnp.where(live, vb[at, :].astype(F32), 0.0).astype(BF16)

    for b in range(side, 2 * side + blocks):
        cache(b)

    @pl.when(jnp.logical_and(jnp.logical_not(upper), has_left))
    def _():
        wait_left()

    attend(peer[1])
    ctx_copy(1).start()
    attend(peer[0])
    mine = pltpu.make_async_copy(
        ctxb.at[me], ctx_out.at[:, pl.ds(pl.multiple_of(me * qw, qw), qw)], loc.at[0])
    mine.start()
    for b in range(side):
        cache(b)
    ck = pltpu.make_async_copy(kst, kc_out, loc.at[1])
    cv = pltpu.make_async_copy(vst, vc_out, loc.at[2])
    ck.start()
    cv.start()

    sib.wait_send()
    for c in range(chunks):
        far_copy(c).wait_send()
        fwd_copy(c).wait_send()

    @pl.when(has_right)
    def _():
        own_copy(0).wait_send()
        for u in rights:
            right_copy(*u).wait_send()

    @pl.when(has_left)
    def _():
        own_copy(1).wait_send()
        for u in lefts:
            left_copy(*u).wait_send()

    mine.wait()
    ck.wait()
    cv.wait()
    for s in (1, 2, 3):
        ctx_copy(s).wait_send()
        pltpu.make_async_remote_copy(
            src_ref=ctxb.at[peer[s]],
            dst_ref=ctx_out.at[:, pl.ds(pl.multiple_of(peer[s] * qw, qw), qw)],
            send_sem=ctx_s.at[s], recv_sem=ctx_r.at[s],
            device_id={"tp": peer[s]}, device_id_type=MESH).wait_recv()


def move(*refs):
    count = len(refs) // 2
    sems = refs[-1]
    copies = [pltpu.make_async_copy(refs[i], refs[count + i], sems.at[i]) for i in range(count)]
    for c in copies:
        c.start()
    for c in copies:
        c.wait()


def shards(n_seq, tp, hidden, norm_gain, w_query, w_key, w_value, doc_start, block_owner):
    rows, width = hidden.shape
    home = doc_start.shape[0]
    qw, kw = w_query.shape[1], w_key.shape[1]
    home_blocks = block_owner.shape[0]
    block_rows = home // home_blocks
    spill = home_blocks // 4 * block_rows
    frame = home + 2 * spill
    assert tp == 4 and spill == rows and DOC_MAX == 2 * rows and rows == HD
    lane = np.arange(HD) % (HD // 2)
    freq = jnp.asarray((ROPE_BASE ** (-2.0 * lane / HD)).astype(np.float32)[None, :])
    nw = qw // kw + 2
    ctx, kc, vc = pl.pallas_call(
        functools.partial(kernel, n_seq, block_rows),
        out_shape=(
            jax.ShapeDtypeStruct((rows, qw * tp), BF16),
            jax.ShapeDtypeStruct((frame, kw), BF16),
            jax.ShapeDtypeStruct((frame, kw), BF16),
        ),
        in_specs=[pl.BlockSpec(memory_space=pltpu.HBM)] * 8,
        out_specs=[pl.BlockSpec(memory_space=pl.ANY)] * 3,
        scratch_shapes=[
            pltpu.VMEM((1, width), F32),
            pltpu.VMEM((tp, rows), jnp.int32),
            pltpu.VMEM((1, home_blocks), jnp.int32),
            pltpu.VMEM((1, HD), F32),
            pltpu.VMEM((3, home_blocks, HD), F32),
            pltpu.VMEM((rows, width), BF16),
            pltpu.VMEM((tp, rows, width), BF16),
            pltpu.VMEM((nw, width, kw), BF16),
            pltpu.VMEM((nw, 2 * rows, kw), F32),
            pltpu.VMEM((nw, 2 * rows // HALVES, kw), F32),
            pltpu.VMEM((home, HD), F32),
            pltpu.VMEM((home, HD), F32),
            pltpu.VMEM((home, HD), F32),
            pltpu.VMEM((home, qw), BF16),
            pltpu.VMEM((DOC_MAX + home + spill, kw), BF16),
            pltpu.VMEM((DOC_MAX + home + spill, kw), BF16),
            pltpu.VMEM((2, 1, home_blocks), jnp.int32),
            pltpu.VMEM((tp, rows, qw), BF16),
            pltpu.VMEM((frame, kw), BF16),
            pltpu.VMEM((frame, kw), BF16),
            pltpu.SemaphoreType.DMA((5 + nw,)),
            pltpu.SemaphoreType.DMA((1,)),
            pltpu.SemaphoreType.DMA((1,)),
            pltpu.SemaphoreType.DMA((HALVES * COLS,)),
            pltpu.SemaphoreType.DMA((HALVES * COLS,)),
            pltpu.SemaphoreType.DMA((HALVES * COLS,)),
            pltpu.SemaphoreType.DMA((HALVES * COLS,)),
            pltpu.SemaphoreType.DMA((4 * HALVES,)),
            pltpu.SemaphoreType.DMA((4 * HALVES,)),
            pltpu.SemaphoreType.DMA((2 * HALVES,)),
            pltpu.SemaphoreType.DMA((2 * HALVES,)),
            pltpu.SemaphoreType.DMA((2,)),
            pltpu.SemaphoreType.DMA((2,)),
            pltpu.SemaphoreType.DMA((4,)),
            pltpu.SemaphoreType.DMA((4,)),
        ],
        compiler_params=pltpu.CompilerParams(
            collective_id=0, has_side_effects=True, vmem_limit_bytes=48 * 1024 * 1024),
    )(*(pltpu.with_memory_space_constraint(a, pltpu.HBM) for a in (
        hidden, norm_gain.reshape(1, width), w_query, w_key, w_value,
        doc_start.reshape(tp, rows),
        block_owner.reshape(1, home_blocks), freq,
    )))
    outs = (ctx, kc, vc)
    return pl.pallas_call(
        move,
        out_shape=tuple(jax.ShapeDtypeStruct(a.shape, a.dtype) for a in outs),
        in_specs=[pl.BlockSpec(memory_space=pl.ANY)] * 3,
        out_specs=[pl.BlockSpec(memory_space=pltpu.HBM)] * 3,
        scratch_shapes=[pltpu.SemaphoreType.DMA((3,))],
        compiler_params=pltpu.CompilerParams(vmem_limit_bytes=1024 * 1024),
    )(*outs)


def solution(mesh):
    return jax.shard_map(
        functools.partial(shards, mesh.shape["seq"], mesh.shape["tp"]),
        mesh=mesh,
        in_specs=(
            P(("seq", "tp"), None), P(), P(None, "tp"), P(None, "tp"), P(None, "tp"),
            P("seq"), P("seq"),
        ),
        out_specs=(P(("seq", "tp"), None), P("seq", "tp"), P("seq", "tp")),
        check_vma=False,
    )
```

```python
import functools

import jax
import jax.numpy as jnp
import numpy as np
from jax import lax
from jax.experimental import pallas as pl
from jax.experimental.pallas import tpu as pltpu
from jax.sharding import PartitionSpec as P

HD = 128
DOC_MAX = 256
EPS = 1e-05
ROPE_BASE = 500000.0
HALVES = 2
COLS = 4
F32 = jnp.float32
BF16 = jnp.bfloat16
MESH = pl.DeviceIdType.MESH


def kernel(
    n_seq, block_rows,
    x_hbm, gain_hbm, wq_hbm, wk_hbm, wv_hbm, doc_hbm, owner_hbm, freq_hbm,
    ctx_out, kc_out, vc_out,
    gain, doc, owner, freq, ownb, xin, hid, w, acc, acc2, cosb, sinb, docb, qb, kb, vb, ob, ctxb, kst, vst,
    loc, sib_s, sib_r, far_s, far_r, fwd_s, fwd_r,
    rt_s, rt_r, lf_s, lf_r, own_s, own_r, ctx_s, ctx_r,
):
    me = lax.axis_index("tp")
    seq = lax.axis_index("seq")
    rows, width = xin.shape
    tp = hid.shape[0]
    home = rows * tp
    reach = DOC_MAX
    spill = kc_out.shape[0] // 2 - home // 2
    half = rows // HALVES
    cw = width // COLS
    first_rows = half // COLS
    kw = kb.shape[1]
    qw = qb.shape[1]
    nw = w.shape[0]
    peer = [me, me + 1 - 2 * (me % 2), (me + 2) % 4, 3 - me]
    has_left = seq > 0
    has_right = seq < n_seq - 1
    upper = me >= 2

    cx = pltpu.make_async_copy(x_hbm, xin, loc.at[0])
    cx.start()
    small = [
        pltpu.make_async_copy(a, b, loc.at[1 + nw + i])
        for i, (a, b) in enumerate(
            ((gain_hbm, gain), (doc_hbm, doc), (owner_hbm, owner), (freq_hbm, freq)))
    ]
    for c in small:
        c.start()
    wcopies = []
    for n in range(nw):
        if n < qw // kw:
            src = wq_hbm.at[:, n * kw:(n + 1) * kw]
        elif n == nw - 2:
            src = wk_hbm
        else:
            src = wv_hbm
        c = pltpu.make_async_copy(src, w.at[n], loc.at[1 + n])
        c.start()
        wcopies.append(c)

    barrier = pltpu.get_barrier_semaphore()
    for s in (1, 2, 3):
        pl.semaphore_signal(barrier, inc=1, device_id={"tp": peer[s]}, device_id_type=MESH)

    @pl.when(has_left)
    def _():
        pl.semaphore_signal(barrier, inc=1, device_id={"seq": seq - 1}, device_id_type=MESH)

    @pl.when(has_right)
    def _():
        pl.semaphore_signal(barrier, inc=1, device_id={"seq": seq + 1}, device_id_type=MESH)

    cx.wait()
    for c in small:
        c.wait()

    def norm_rows(i, carry):
        at = pl.ds(pl.multiple_of(i * 16, 16), 16)
        wide = xin[at, :].astype(F32)
        inv = lax.rsqrt(jnp.mean(wide * wide, axis=1, keepdims=True) + EPS)
        hid[0, at, :] = (wide * inv * gain[...]).astype(BF16)
        return carry

    def part(slot, c):
        h, k = c // COLS, c % COLS
        if h == 0:
            return hid.at[slot, pl.ds(k * first_rows, first_rows), :]
        return hid.at[slot, pl.ds(h * half, half), pl.ds(k * cw, cw)]

    def far_copy(c):
        return pltpu.make_async_remote_copy(
            src_ref=part(0, c), dst_ref=part(2, c), send_sem=far_s.at[c], recv_sem=far_r.at[c],
            device_id={"tp": peer[2]}, device_id_type=MESH)

    def fwd_copy(c):
        return pltpu.make_async_remote_copy(
            src_ref=part(2, c), dst_ref=part(3, c), send_sem=fwd_s.at[c], recv_sem=fwd_r.at[c],
            device_id={"tp": peer[1]}, device_id_type=MESH)

    sib = pltpu.make_async_remote_copy(
        src_ref=hid.at[0], dst_ref=hid.at[1], send_sem=sib_s.at[0], recv_sem=sib_r.at[0],
        device_id={"tp": peer[1]}, device_id_type=MESH)
    chunks = HALVES * COLS
    lax.fori_loop(0, first_rows // 16, norm_rows, 0)
    pl.semaphore_wait(barrier, 3 + has_left.astype(jnp.int32) + has_right.astype(jnp.int32))
    far_copy(0).start()
    for c in range(1, COLS):
        lax.fori_loop(c * (first_rows // 16), (c + 1) * (first_rows // 16), norm_rows, 0)
        far_copy(c).start()
    lax.fori_loop(half // 16, rows // 16, norm_rows, 0)
    for c in range(COLS, chunks):
        far_copy(c).start()
    sib.start()

    def own_copy(d):
        return pltpu.make_async_remote_copy(
            src_ref=owner, dst_ref=ob.at[d], send_sem=own_s.at[d], recv_sem=own_r.at[d],
            device_id={"seq": seq + 1 if d == 0 else seq - 1}, device_id_type=MESH)

    kv = (kb, vb)

    def right_copy(t, b, h):
        u = (t * 2 + b) * HALVES + h
        lo = b * rows + h * half
        return pltpu.make_async_remote_copy(
            src_ref=kv[t].at[pl.ds(home + lo, half)], dst_ref=kv[t].at[pl.ds(lo, half)],
            send_sem=rt_s.at[u], recv_sem=rt_r.at[u],
            device_id={"seq": seq + 1}, device_id_type=MESH)

    def left_copy(t, h):
        u = t * HALVES + h
        return pltpu.make_async_remote_copy(
            src_ref=kv[t].at[pl.ds(reach + h * half, half)],
            dst_ref=kv[t].at[pl.ds(reach + home + h * half, half)],
            send_sem=lf_s.at[u], recv_sem=lf_r.at[u],
            device_id={"seq": seq - 1}, device_id_type=MESH)

    rights = [(t, b, h) for h in range(HALVES) for t in range(2) for b in range(2)]
    lefts = [(t, h) for h in range(HALVES) for t in range(2)]

    @pl.when(has_right)
    def _():
        own_copy(0).start()

    @pl.when(has_left)
    def _():
        own_copy(1).start()

    @pl.when(jnp.logical_not(has_left))
    def _():
        kb[pl.ds(0, reach), :] = jnp.zeros((reach, kw), BF16)
        vb[pl.ds(0, reach), :] = jnp.zeros((reach, kw), BF16)
        ob[0] = jnp.full(owner.shape, -1, jnp.int32)

    @pl.when(jnp.logical_not(has_right))
    def _():
        kb[pl.ds(reach + home, spill), :] = jnp.zeros((spill, kw), BF16)
        vb[pl.ds(reach + home, spill), :] = jnp.zeros((spill, kw), BF16)
        ob[1] = jnp.full(owner.shape, -1, jnp.int32)

    row_i = lax.broadcasted_iota(jnp.int32, (rows, rows), 0)
    col_i = lax.broadcasted_iota(jnp.int32, (rows, rows), 1)
    first = (seq * home).astype(F32)
    for j in range(tp):
        line = jnp.broadcast_to(doc[j:j + 1, :].astype(F32) - first, (rows, rows))
        column = jnp.sum(jnp.where(row_i == col_i, line, 0.0), axis=1, keepdims=True)
        start = jnp.broadcast_to(column, (rows, rows))
        docb[j * rows:(j + 1) * rows, :] = start
        angle = (row_i.astype(F32) + float(j * rows) - start) * freq[...]
        cosb[j * rows:(j + 1) * rows, :] = jnp.cos(angle)
        sine = jnp.sin(angle)
        sinb[j * rows:(j + 1) * rows, :] = jnp.where(col_i < HD // 2, -sine, sine)

    def turned(ref, n, e, src_row, count, at):
        y = ref[n, src_row:src_row + count, e * HD:(e + 1) * HD]
        cos = cosb[pl.ds(at, count), :]
        sin = sinb[pl.ds(at, count), :]
        return (y * cos + pltpu.roll(y, HD // 2, 1) * sin).astype(BF16)

    def finish_kv(ref, src_row, count, at):
        put = pl.ds(at + reach, count)
        for e in range(kw // HD):
            kb[put, e * HD:(e + 1) * HD] = turned(ref, nw - 2, e, src_row, count, at)
        vb[put, :] = ref[nw - 1, src_row:src_row + count, :].astype(BF16)

    def finish_q(ref, src_row, count, at):
        for n in range(nw - 2):
            for e in range(kw // HD):
                lane = n * kw + e * HD
                qb[pl.ds(at, count), lane:lane + HD] = turned(ref, n, e, src_row, count, at)

    for c in wcopies:
        c.wait()
    sib.wait_recv()

    def early(n, carry):
        lhs = hid[0:2].reshape(2 * rows, width)
        acc[n] = jnp.dot(lhs, w[n], preferred_element_type=F32)
        return carry

    def place(s, h=0):
        return pl.multiple_of(peer[s] * rows + h * half, half)

    lax.fori_loop(nw - 2, nw, early, 0)
    for s in range(2):
        finish_kv(acc, s * rows, rows, place(s))

    @pl.when(jnp.logical_and(upper, has_right))
    def _():
        for u in rights:
            right_copy(*u).start()

    @pl.when(jnp.logical_and(jnp.logical_not(upper), has_left))
    def _():
        for u in lefts:
            left_copy(*u).start()

    lax.fori_loop(0, nw - 2, early, 0)
    for s in range(2):
        finish_q(acc, s * rows, rows, place(s))

    def send_kv(h):
        for s in range(2):
            finish_kv(acc2, s * half, half, place(2 + s, h))

        @pl.when(jnp.logical_and(jnp.logical_not(upper), has_right))
        def _():
            for u in rights:
                if u[-1] == h:
                    right_copy(*u).start()

        @pl.when(jnp.logical_and(upper, has_left))
        def _():
            for u in lefts:
                if u[-1] == h:
                    left_copy(*u).start()

    def wait_left():
        for u in rights:
            right_copy(*u).wait_recv()

    groups = kw // HD
    per = qw // kw

    def attend(j, at, count):
        window = count + reach
        base = pl.multiple_of(j * rows + at, half)
        ci = lax.broadcasted_iota(jnp.int32, (count, window), 1)
        ri = lax.broadcasted_iota(jnp.int32, (count, window), 0)
        start = jnp.broadcast_to(docb[pl.ds(base, count), 0:1], (count, window))
        local = (ci + (base - reach)).astype(F32)
        allowed = jnp.logical_and(local >= start, ci <= ri + reach)
        allowed = jnp.concatenate([allowed] * per, axis=0)
        for g in range(groups):
            q = jnp.concatenate(
                [qb[pl.ds(base, count), (g * per + e) * HD:(g * per + e + 1) * HD] for e in range(per)], axis=0)
            keys = kb[pl.ds(base, window), g * HD:(g + 1) * HD]
            vals = vb[pl.ds(base, window), g * HD:(g + 1) * HD]
            sc = lax.dot_general(q, keys, (((1,), (1,)), ((), ())), preferred_element_type=F32) * HD ** (-0.5)
            sc = jnp.where(allowed, sc, -jnp.inf)
            ex = jnp.exp(sc - jnp.max(sc, axis=1, keepdims=True))
            wt = (ex * (1.0 / jnp.sum(ex, axis=1, keepdims=True))).astype(BF16)
            o = jnp.dot(wt, vals, preferred_element_type=F32).astype(BF16)
            for e in range(per):
                ctxb[j, at:at + count, (g * per + e) * HD:(g * per + e + 1) * HD] = o[e * count:(e + 1) * count]

    def ctx_copy(to, slot, h, count, whose):
        at = pl.ds(h * half, count)
        return pltpu.make_async_remote_copy(
            src_ref=ctxb.at[to, at],
            dst_ref=ctx_out.at[at, pl.ds(pl.multiple_of(whose * qw, qw), qw)],
            send_sem=ctx_s.at[slot * HALVES + h], recv_sem=ctx_r.at[slot * HALVES + h],
            device_id={"tp": to}, device_id_type=MESH)

    low = 2 - 2 * (me // 2)
    low_slot = 2 + me % 2
    far_of = ((low, low_slot), (low + 1, 5 - low_slot))

    for c in range(COLS):
        far_copy(c).wait_recv()
        fwd_copy(c).start()
    for c in range(COLS):
        fwd_copy(c).wait_recv()

    def late_first(n, carry):
        lhs = hid[2:4, 0:half, :].reshape(2 * half, width)
        acc2[n] = jnp.dot(lhs, w[n], preferred_element_type=F32)
        return carry

    lax.fori_loop(nw - 2, nw, late_first, 0)
    send_kv(0)
    lax.fori_loop(0, nw - 2, late_first, 0)
    for s in range(2):
        finish_q(acc2, s * half, half, place(2 + s, 0))

    @pl.when(jnp.logical_and(upper, has_left))
    def _():
        wait_left()

    attend(low, 0, half)
    ctx_copy(low, low_slot, 0, half, me).start()

    for k in range(COLS):
        c = COLS + k
        far_copy(c).wait_recv()
        fwd_copy(c).start()
        fwd_copy(c).wait_recv()

        def late(n, carry):
            lhs = hid[2:4, half:2 * half, k * cw:(k + 1) * cw].reshape(2 * half, cw)
            got = jnp.dot(lhs, w[n, k * cw:(k + 1) * cw, :], preferred_element_type=F32)
            if k == 0:
                acc2[n] = got
            else:
                acc2[n] += got
            return carry

        lax.fori_loop(nw - 2, nw, late, 0)
        if k == COLS - 1:
            send_kv(1)
        lax.fori_loop(0, nw - 2, late, 0)
    for s in range(2):
        finish_q(acc2, s * half, half, place(2 + s, 1))

    for (to, slot), h in ((far_of[0], 1), (far_of[1], 0), (far_of[1], 1)):
        attend(to, h * half, half)
        ctx_copy(to, slot, h, half, me).start()

    @pl.when(has_right)
    def _():
        own_copy(1).wait_recv()
        for u in lefts:
            left_copy(*u).wait_recv()

    @pl.when(has_left)
    def _():
        own_copy(0).wait_recv()

    side = spill // block_rows
    blocks = home // block_rows
    eye = (lax.broadcasted_iota(jnp.int32, (blocks, blocks), 0)
           == lax.broadcasted_iota(jnp.int32, (blocks, blocks), 1))
    for i in range(3):
        line = owner[...] if i == 1 else ob[i // 2]
        line = jnp.broadcast_to(line.astype(F32), (blocks, blocks))
        column = jnp.sum(jnp.where(eye, line, 0.0), axis=1, keepdims=True)
        ownb[i] = jnp.broadcast_to(column, (blocks, HD))
    seq_f = seq.astype(F32)

    def cache(b):
        if b < side:
            line = ownb[0, blocks - side + b:blocks - side + b + 1, :]
        elif b < side + blocks:
            line = ownb[1, b - side:b - side + 1, :]
        else:
            line = ownb[2, b - side - blocks:b - side - blocks + 1, :]
        line = jnp.broadcast_to(jnp.where(line == seq_f, 1.0, 0.0), (block_rows, HD))
        live = jnp.concatenate([line] * (kw // HD), axis=1) > 0.5
        to = slice(b * block_rows, (b + 1) * block_rows)
        at = slice(reach - spill + b * block_rows, reach - spill + (b + 1) * block_rows)
        kst[to, :] = jnp.where(live, kb[at, :].astype(F32), 0.0).astype(BF16)
        vst[to, :] = jnp.where(live, vb[at, :].astype(F32), 0.0).astype(BF16)

    for b in range(side, 2 * side + blocks):
        cache(b)

    @pl.when(jnp.logical_and(jnp.logical_not(upper), has_left))
    def _():
        wait_left()

    attend(peer[1], 0, rows)
    ctx_copy(peer[1], 1, 0, rows, me).start()
    attend(peer[0], 0, rows)
    mine = pltpu.make_async_copy(
        ctxb.at[me], ctx_out.at[:, pl.ds(pl.multiple_of(me * qw, qw), qw)], loc.at[0])
    mine.start()
    for b in range(side):
        cache(b)
    ck = pltpu.make_async_copy(kst, kc_out, loc.at[1])
    cv = pltpu.make_async_copy(vst, vc_out, loc.at[2])
    ck.start()
    cv.start()

    sib.wait_send()
    for c in range(chunks):
        far_copy(c).wait_send()
        fwd_copy(c).wait_send()

    @pl.when(has_right)
    def _():
        own_copy(0).wait_send()
        for u in rights:
            right_copy(*u).wait_send()

    @pl.when(has_left)
    def _():
        own_copy(1).wait_send()
        for u in lefts:
            left_copy(*u).wait_send()

    mine.wait()
    ck.wait()
    cv.wait()
    ctx_copy(peer[1], 1, 0, rows, me).wait_send()
    ctx_copy(peer[1], 1, 0, rows, peer[1]).wait_recv()
    for s in (2, 3):
        for h in range(HALVES):
            ctx_copy(peer[s], s, h, half, me).wait_send()
            ctx_copy(peer[s], s, h, half, peer[s]).wait_recv()


def move(*refs):
    count = len(refs) // 2
    sems = refs[-1]
    copies = [pltpu.make_async_copy(refs[i], refs[count + i], sems.at[i]) for i in range(count)]
    for c in copies:
        c.start()
    for c in copies:
        c.wait()


def shards(n_seq, tp, hidden, norm_gain, w_query, w_key, w_value, doc_start, block_owner):
    rows, width = hidden.shape
    home = doc_start.shape[0]
    qw, kw = w_query.shape[1], w_key.shape[1]
    home_blocks = block_owner.shape[0]
    block_rows = home // home_blocks
    spill = home_blocks // 4 * block_rows
    frame = home + 2 * spill
    assert tp == 4 and spill == rows and DOC_MAX == 2 * rows and rows == HD
    lane = np.arange(HD) % (HD // 2)
    freq = jnp.asarray((ROPE_BASE ** (-2.0 * lane / HD)).astype(np.float32)[None, :])
    nw = qw // kw + 2
    ctx, kc, vc = pl.pallas_call(
        functools.partial(kernel, n_seq, block_rows),
        out_shape=(
            jax.ShapeDtypeStruct((rows, qw * tp), BF16),
            jax.ShapeDtypeStruct((frame, kw), BF16),
            jax.ShapeDtypeStruct((frame, kw), BF16),
        ),
        in_specs=[pl.BlockSpec(memory_space=pltpu.HBM)] * 8,
        out_specs=[pl.BlockSpec(memory_space=pl.ANY)] * 3,
        scratch_shapes=[
            pltpu.VMEM((1, width), F32),
            pltpu.VMEM((tp, rows), jnp.int32),
            pltpu.VMEM((1, home_blocks), jnp.int32),
            pltpu.VMEM((1, HD), F32),
            pltpu.VMEM((3, home_blocks, HD), F32),
            pltpu.VMEM((rows, width), BF16),
            pltpu.VMEM((tp, rows, width), BF16),
            pltpu.VMEM((nw, width, kw), BF16),
            pltpu.VMEM((nw, 2 * rows, kw), F32),
            pltpu.VMEM((nw, 2 * rows // HALVES, kw), F32),
            pltpu.VMEM((home, HD), F32),
            pltpu.VMEM((home, HD), F32),
            pltpu.VMEM((home, HD), F32),
            pltpu.VMEM((home, qw), BF16),
            pltpu.VMEM((DOC_MAX + home + spill, kw), BF16),
            pltpu.VMEM((DOC_MAX + home + spill, kw), BF16),
            pltpu.VMEM((2, 1, home_blocks), jnp.int32),
            pltpu.VMEM((tp, rows, qw), BF16),
            pltpu.VMEM((frame, kw), BF16),
            pltpu.VMEM((frame, kw), BF16),
            pltpu.SemaphoreType.DMA((5 + nw,)),
            pltpu.SemaphoreType.DMA((1,)),
            pltpu.SemaphoreType.DMA((1,)),
            pltpu.SemaphoreType.DMA((HALVES * COLS,)),
            pltpu.SemaphoreType.DMA((HALVES * COLS,)),
            pltpu.SemaphoreType.DMA((HALVES * COLS,)),
            pltpu.SemaphoreType.DMA((HALVES * COLS,)),
            pltpu.SemaphoreType.DMA((4 * HALVES,)),
            pltpu.SemaphoreType.DMA((4 * HALVES,)),
            pltpu.SemaphoreType.DMA((2 * HALVES,)),
            pltpu.SemaphoreType.DMA((2 * HALVES,)),
            pltpu.SemaphoreType.DMA((2,)),
            pltpu.SemaphoreType.DMA((2,)),
            pltpu.SemaphoreType.DMA((4 * HALVES,)),
            pltpu.SemaphoreType.DMA((4 * HALVES,)),
        ],
        compiler_params=pltpu.CompilerParams(
            collective_id=0, has_side_effects=True, vmem_limit_bytes=48 * 1024 * 1024),
    )(*(pltpu.with_memory_space_constraint(a, pltpu.HBM) for a in (
        hidden, norm_gain.reshape(1, width), w_query, w_key, w_value,
        doc_start.reshape(tp, rows),
        block_owner.reshape(1, home_blocks), freq,
    )))
    outs = (ctx, kc, vc)
    return pl.pallas_call(
        move,
        out_shape=tuple(jax.ShapeDtypeStruct(a.shape, a.dtype) for a in outs),
        in_specs=[pl.BlockSpec(memory_space=pl.ANY)] * 3,
        out_specs=[pl.BlockSpec(memory_space=pltpu.HBM)] * 3,
        scratch_shapes=[pltpu.SemaphoreType.DMA((3,))],
        compiler_params=pltpu.CompilerParams(vmem_limit_bytes=1024 * 1024),
    )(*outs)


def solution(mesh):
    return jax.shard_map(
        functools.partial(shards, mesh.shape["seq"], mesh.shape["tp"]),
        mesh=mesh,
        in_specs=(
            P(("seq", "tp"), None), P(), P(None, "tp"), P(None, "tp"), P(None, "tp"),
            P("seq"), P("seq"),
        ),
        out_specs=(P(("seq", "tp"), None), P("seq", "tp"), P("seq", "tp")),
        check_vma=False,
    )
```

```python
import functools

import jax
import jax.numpy as jnp
import numpy as np
from jax import lax
from jax.experimental import pallas as pl
from jax.experimental.pallas import tpu as pltpu
from jax.sharding import PartitionSpec as P

HD = 128
DOC_MAX = 256
EPS = 1e-05
ROPE_BASE = 500000.0
HALVES = 2
COLS = 4
PIECES = 4
F32 = jnp.float32
BF16 = jnp.bfloat16
MESH = pl.DeviceIdType.MESH


def kernel(
    n_seq, block_rows,
    x_hbm, gain_hbm, wq_hbm, wk_hbm, wv_hbm, doc_hbm, owner_hbm, freq_hbm,
    ctx_out, kc_out, vc_out,
    gain, doc, owner, freq, ownb, xin, hid, w, acc, acc2, cosb, sinb, docb, qb, kb, vb, ob, ctxb, kst, vst,
    loc, sib_s, sib_r, far_s, far_r, fwd_s, fwd_r,
    rt_s, rt_r, lf_s, lf_r, own_s, own_r, ctx_s, ctx_r,
):
    me = lax.axis_index("tp")
    seq = lax.axis_index("seq")
    rows, width = xin.shape
    tp = hid.shape[0]
    home = rows * tp
    reach = DOC_MAX
    spill = kc_out.shape[0] // 2 - home // 2
    half = rows // HALVES
    cw = width // COLS
    first_rows = half // COLS
    kw = kb.shape[1]
    qw = qb.shape[1]
    nw = w.shape[0]
    peer = [me, me + 1 - 2 * (me % 2), (me + 2) % 4, 3 - me]
    has_left = seq > 0
    has_right = seq < n_seq - 1
    upper = me >= 2

    lead = half // COLS
    cx0 = pltpu.make_async_copy(x_hbm.at[pl.ds(0, lead)], xin.at[pl.ds(0, lead)], loc.at[5 + nw])
    cx = pltpu.make_async_copy(
        x_hbm.at[pl.ds(lead, rows - lead)], xin.at[pl.ds(lead, rows - lead)], loc.at[0])
    cx0.start()
    small = [
        pltpu.make_async_copy(a, b, loc.at[1 + nw + i])
        for i, (a, b) in enumerate(
            ((gain_hbm, gain), (doc_hbm, doc), (owner_hbm, owner), (freq_hbm, freq)))
    ]
    for c in small:
        c.start()
    cx.start()
    wcopies = []
    for n in range(nw):
        if n < qw // kw:
            src = wq_hbm.at[:, n * kw:(n + 1) * kw]
        elif n == nw - 2:
            src = wk_hbm
        else:
            src = wv_hbm
        wcopies.append(pltpu.make_async_copy(src, w.at[n], loc.at[1 + n]))

    barrier = pltpu.get_barrier_semaphore()
    for s in (1, 2, 3):
        pl.semaphore_signal(barrier, inc=1, device_id={"tp": peer[s]}, device_id_type=MESH)

    @pl.when(has_left)
    def _():
        pl.semaphore_signal(barrier, inc=1, device_id={"seq": seq - 1}, device_id_type=MESH)

    @pl.when(has_right)
    def _():
        pl.semaphore_signal(barrier, inc=1, device_id={"seq": seq + 1}, device_id_type=MESH)

    cx0.wait()
    for c in small:
        c.wait()

    def norm_rows(i, carry):
        at = pl.ds(pl.multiple_of(i * 16, 16), 16)
        wide = xin[at, :].astype(F32)
        inv = lax.rsqrt(jnp.mean(wide * wide, axis=1, keepdims=True) + EPS)
        hid[0, at, :] = (wide * inv * gain[...]).astype(BF16)
        return carry

    def part(slot, c):
        h, k = c // COLS, c % COLS
        if h == 0:
            return hid.at[slot, pl.ds(k * first_rows, first_rows), :]
        return hid.at[slot, pl.ds(h * half, half), pl.ds(k * cw, cw)]

    def far_copy(c):
        return pltpu.make_async_remote_copy(
            src_ref=part(0, c), dst_ref=part(2, c), send_sem=far_s.at[c], recv_sem=far_r.at[c],
            device_id={"tp": peer[2]}, device_id_type=MESH)

    def fwd_copy(c):
        return pltpu.make_async_remote_copy(
            src_ref=part(2, c), dst_ref=part(3, c), send_sem=fwd_s.at[c], recv_sem=fwd_r.at[c],
            device_id={"tp": peer[1]}, device_id_type=MESH)

    sib = pltpu.make_async_remote_copy(
        src_ref=hid.at[0], dst_ref=hid.at[1], send_sem=sib_s.at[0], recv_sem=sib_r.at[0],
        device_id={"tp": peer[1]}, device_id_type=MESH)
    chunks = HALVES * COLS
    lax.fori_loop(0, first_rows // 16, norm_rows, 0)
    pl.semaphore_wait(barrier, 3 + has_left.astype(jnp.int32) + has_right.astype(jnp.int32))
    far_copy(0).start()
    cx.wait()
    for c in wcopies:
        c.start()
    for c in range(1, COLS):
        lax.fori_loop(c * (first_rows // 16), (c + 1) * (first_rows // 16), norm_rows, 0)
        far_copy(c).start()
    lax.fori_loop(half // 16, rows // 16, norm_rows, 0)
    for c in range(COLS, chunks):
        far_copy(c).start()
    sib.start()

    def own_copy(d):
        return pltpu.make_async_remote_copy(
            src_ref=owner, dst_ref=ob.at[d], send_sem=own_s.at[d], recv_sem=own_r.at[d],
            device_id={"seq": seq + 1 if d == 0 else seq - 1}, device_id_type=MESH)

    kv = (kb, vb)

    def right_copy(t, b, h):
        u = (t * 2 + b) * HALVES + h
        lo = b * rows + h * half
        return pltpu.make_async_remote_copy(
            src_ref=kv[t].at[pl.ds(home + lo, half)], dst_ref=kv[t].at[pl.ds(lo, half)],
            send_sem=rt_s.at[u], recv_sem=rt_r.at[u],
            device_id={"seq": seq + 1}, device_id_type=MESH)

    def left_copy(t, h):
        u = t * HALVES + h
        return pltpu.make_async_remote_copy(
            src_ref=kv[t].at[pl.ds(reach + h * half, half)],
            dst_ref=kv[t].at[pl.ds(reach + home + h * half, half)],
            send_sem=lf_s.at[u], recv_sem=lf_r.at[u],
            device_id={"seq": seq - 1}, device_id_type=MESH)

    rights = [(t, b, h) for h in range(HALVES) for t in range(2) for b in range(2)]
    lefts = [(t, h) for h in range(HALVES) for t in range(2)]

    @pl.when(has_right)
    def _():
        own_copy(0).start()

    @pl.when(has_left)
    def _():
        own_copy(1).start()

    @pl.when(jnp.logical_not(has_left))
    def _():
        kb[pl.ds(0, reach), :] = jnp.zeros((reach, kw), BF16)
        vb[pl.ds(0, reach), :] = jnp.zeros((reach, kw), BF16)
        ob[0] = jnp.full(owner.shape, -1, jnp.int32)

    @pl.when(jnp.logical_not(has_right))
    def _():
        kb[pl.ds(reach + home, spill), :] = jnp.zeros((spill, kw), BF16)
        vb[pl.ds(reach + home, spill), :] = jnp.zeros((spill, kw), BF16)
        ob[1] = jnp.full(owner.shape, -1, jnp.int32)

    row_i = lax.broadcasted_iota(jnp.int32, (rows, rows), 0)
    col_i = lax.broadcasted_iota(jnp.int32, (rows, rows), 1)
    first = (seq * home).astype(F32)
    for j in range(tp):
        line = jnp.broadcast_to(doc[j:j + 1, :].astype(F32) - first, (rows, rows))
        column = jnp.sum(jnp.where(row_i == col_i, line, 0.0), axis=1, keepdims=True)
        start = jnp.broadcast_to(column, (rows, rows))
        docb[j * rows:(j + 1) * rows, :] = start
        angle = (row_i.astype(F32) + float(j * rows) - start) * freq[...]
        cosb[j * rows:(j + 1) * rows, :] = jnp.cos(angle)
        sine = jnp.sin(angle)
        sinb[j * rows:(j + 1) * rows, :] = jnp.where(col_i < HD // 2, -sine, sine)

    def turned(ref, n, e, src_row, count, at):
        y = ref[n, src_row:src_row + count, e * HD:(e + 1) * HD]
        cos = cosb[pl.ds(at, count), :]
        sin = sinb[pl.ds(at, count), :]
        return (y * cos + pltpu.roll(y, HD // 2, 1) * sin).astype(BF16)

    def finish_kv(ref, src_row, count, at):
        put = pl.ds(at + reach, count)
        for e in range(kw // HD):
            kb[put, e * HD:(e + 1) * HD] = turned(ref, nw - 2, e, src_row, count, at)
        vb[put, :] = ref[nw - 1, src_row:src_row + count, :].astype(BF16)

    def finish_q(ref, src_row, count, at):
        for n in range(nw - 2):
            for e in range(kw // HD):
                lane = n * kw + e * HD
                qb[pl.ds(at, count), lane:lane + HD] = turned(ref, n, e, src_row, count, at)

    for c in wcopies:
        c.wait()
    sib.wait_recv()

    def early(n, carry):
        lhs = hid[0:2].reshape(2 * rows, width)
        acc[n] = jnp.dot(lhs, w[n], preferred_element_type=F32)
        return carry

    def place(s, h=0):
        return pl.multiple_of(peer[s] * rows + h * half, half)

    lax.fori_loop(nw - 2, nw, early, 0)
    for s in range(2):
        finish_kv(acc, s * rows, rows, place(s))

    @pl.when(jnp.logical_and(upper, has_right))
    def _():
        for u in rights:
            right_copy(*u).start()

    @pl.when(jnp.logical_and(jnp.logical_not(upper), has_left))
    def _():
        for u in lefts:
            left_copy(*u).start()

    lax.fori_loop(0, nw - 2, early, 0)
    for s in range(2):
        finish_q(acc, s * rows, rows, place(s))

    def send_kv(h):
        for s in range(2):
            finish_kv(acc2, s * half, half, place(2 + s, h))

        @pl.when(jnp.logical_and(jnp.logical_not(upper), has_right))
        def _():
            for u in rights:
                if u[-1] == h:
                    right_copy(*u).start()

        @pl.when(jnp.logical_and(upper, has_left))
        def _():
            for u in lefts:
                if u[-1] == h:
                    left_copy(*u).start()

    def wait_left():
        for u in rights:
            right_copy(*u).wait_recv()

    groups = kw // HD
    per = qw // kw

    def attend(j, at, count):
        window = count + reach
        base = pl.multiple_of(j * rows + at, half)
        ci = lax.broadcasted_iota(jnp.int32, (count, window), 1)
        ri = lax.broadcasted_iota(jnp.int32, (count, window), 0)
        start = jnp.broadcast_to(docb[pl.ds(base, count), 0:1], (count, window))
        local = (ci + (base - reach)).astype(F32)
        allowed = jnp.logical_and(local >= start, ci <= ri + reach)
        allowed = jnp.concatenate([allowed] * per, axis=0)
        for g in range(groups):
            q = jnp.concatenate(
                [qb[pl.ds(base, count), (g * per + e) * HD:(g * per + e + 1) * HD] for e in range(per)], axis=0)
            keys = kb[pl.ds(base, window), g * HD:(g + 1) * HD]
            vals = vb[pl.ds(base, window), g * HD:(g + 1) * HD]
            sc = lax.dot_general(q, keys, (((1,), (1,)), ((), ())), preferred_element_type=F32) * HD ** (-0.5)
            sc = jnp.where(allowed, sc, -jnp.inf)
            ex = jnp.exp(sc - jnp.max(sc, axis=1, keepdims=True))
            wt = (ex * (1.0 / jnp.sum(ex, axis=1, keepdims=True))).astype(BF16)
            o = jnp.dot(wt, vals, preferred_element_type=F32).astype(BF16)
            for e in range(per):
                ctxb[j, at:at + count, (g * per + e) * HD:(g * per + e + 1) * HD] = o[e * count:(e + 1) * count]

    def ctx_copy(to, slot, h, count, whose):
        at = pl.ds(h * half, count)
        return pltpu.make_async_remote_copy(
            src_ref=ctxb.at[to, at],
            dst_ref=ctx_out.at[at, pl.ds(pl.multiple_of(whose * qw, qw), qw)],
            send_sem=ctx_s.at[slot * HALVES + h], recv_sem=ctx_r.at[slot * HALVES + h],
            device_id={"tp": to}, device_id_type=MESH)

    low = 2 - 2 * (me // 2)
    low_slot = 2 + me % 2
    far_of = ((low, low_slot), (low + 1, 5 - low_slot))

    for c in range(COLS):
        far_copy(c).wait_recv()
        fwd_copy(c).start()
    for c in range(COLS):
        fwd_copy(c).wait_recv()

    def late_first(n, carry):
        lhs = hid[2:4, 0:half, :].reshape(2 * half, width)
        acc2[n] = jnp.dot(lhs, w[n], preferred_element_type=F32)
        return carry

    lax.fori_loop(nw - 2, nw, late_first, 0)
    send_kv(0)
    lax.fori_loop(0, nw - 2, late_first, 0)
    for s in range(2):
        finish_q(acc2, s * half, half, place(2 + s, 0))

    @pl.when(jnp.logical_and(upper, has_left))
    def _():
        wait_left()

    attend(low, 0, half)
    ctx_copy(low, low_slot, 0, half, me).start()

    for k in range(COLS):
        c = COLS + k
        far_copy(c).wait_recv()
        fwd_copy(c).start()
        fwd_copy(c).wait_recv()

        def late(n, carry):
            lhs = hid[2:4, half:2 * half, k * cw:(k + 1) * cw].reshape(2 * half, cw)
            got = jnp.dot(lhs, w[n, k * cw:(k + 1) * cw, :], preferred_element_type=F32)
            if k == 0:
                acc2[n] = got
            else:
                acc2[n] += got
            return carry

        lax.fori_loop(nw - 2, nw, late, 0)
        if k == COLS - 1:
            send_kv(1)
        lax.fori_loop(0, nw - 2, late, 0)
    for s in range(2):
        finish_q(acc2, s * half, half, place(2 + s, 1))

    for (to, slot), h in ((far_of[0], 1), (far_of[1], 0), (far_of[1], 1)):
        attend(to, h * half, half)
        ctx_copy(to, slot, h, half, me).start()

    @pl.when(has_right)
    def _():
        own_copy(1).wait_recv()
        for u in lefts:
            left_copy(*u).wait_recv()

    @pl.when(has_left)
    def _():
        own_copy(0).wait_recv()

    side = spill // block_rows
    blocks = home // block_rows
    eye = (lax.broadcasted_iota(jnp.int32, (blocks, blocks), 0)
           == lax.broadcasted_iota(jnp.int32, (blocks, blocks), 1))
    for i in range(3):
        line = owner[...] if i == 1 else ob[i // 2]
        line = jnp.broadcast_to(line.astype(F32), (blocks, blocks))
        column = jnp.sum(jnp.where(eye, line, 0.0), axis=1, keepdims=True)
        ownb[i] = jnp.broadcast_to(column, (blocks, HD))
    seq_f = seq.astype(F32)

    def cache(b):
        if b < side:
            line = ownb[0, blocks - side + b:blocks - side + b + 1, :]
        elif b < side + blocks:
            line = ownb[1, b - side:b - side + 1, :]
        else:
            line = ownb[2, b - side - blocks:b - side - blocks + 1, :]
        line = jnp.broadcast_to(jnp.where(line == seq_f, 1.0, 0.0), (block_rows, HD))
        live = jnp.concatenate([line] * (kw // HD), axis=1) > 0.5
        to = slice(b * block_rows, (b + 1) * block_rows)
        at = slice(reach - spill + b * block_rows, reach - spill + (b + 1) * block_rows)
        kst[to, :] = jnp.where(live, kb[at, :].astype(F32), 0.0).astype(BF16)
        vst[to, :] = jnp.where(live, vb[at, :].astype(F32), 0.0).astype(BF16)

    for b in range(side, 2 * side + blocks):
        cache(b)

    @pl.when(jnp.logical_and(jnp.logical_not(upper), has_left))
    def _():
        wait_left()

    attend(peer[1], 0, rows)
    ctx_copy(peer[1], 1, 0, rows, me).start()
    attend(peer[0], 0, rows)
    mine = pltpu.make_async_copy(
        ctxb.at[me], ctx_out.at[:, pl.ds(pl.multiple_of(me * qw, qw), qw)], loc.at[0])
    mine.start()
    for b in range(side):
        cache(b)
    ck = pltpu.make_async_copy(kst, kc_out, loc.at[1])
    cv = pltpu.make_async_copy(vst, vc_out, loc.at[2])
    ck.start()
    cv.start()

    sib.wait_send()
    for c in range(chunks):
        far_copy(c).wait_send()
        fwd_copy(c).wait_send()

    @pl.when(has_right)
    def _():
        own_copy(0).wait_send()
        for u in rights:
            right_copy(*u).wait_send()

    @pl.when(has_left)
    def _():
        own_copy(1).wait_send()
        for u in lefts:
            left_copy(*u).wait_send()

    mine.wait()
    ck.wait()
    cv.wait()
    ctx_copy(peer[1], 1, 0, rows, me).wait_send()
    ctx_copy(peer[1], 1, 0, rows, peer[1]).wait_recv()
    for s in (2, 3):
        for h in range(HALVES):
            ctx_copy(peer[s], s, h, half, me).wait_send()
            ctx_copy(peer[s], s, h, half, peer[s]).wait_recv()


def move(*refs):
    count = len(refs) // 2
    sems = refs[-1]
    copies = []
    for i in range(count):
        step = refs[i].shape[0] // PIECES
        for p in range(PIECES):
            at = pl.ds(p * step, step)
            copies.append(pltpu.make_async_copy(
                refs[i].at[at], refs[count + i].at[at], sems.at[i * PIECES + p]))
    for c in copies:
        c.start()
    for c in copies:
        c.wait()


def shards(n_seq, tp, hidden, norm_gain, w_query, w_key, w_value, doc_start, block_owner):
    rows, width = hidden.shape
    home = doc_start.shape[0]
    qw, kw = w_query.shape[1], w_key.shape[1]
    home_blocks = block_owner.shape[0]
    block_rows = home // home_blocks
    spill = home_blocks // 4 * block_rows
    frame = home + 2 * spill
    assert tp == 4 and spill == rows and DOC_MAX == 2 * rows and rows == HD
    lane = np.arange(HD) % (HD // 2)
    freq = jnp.asarray((ROPE_BASE ** (-2.0 * lane / HD)).astype(np.float32)[None, :])
    nw = qw // kw + 2
    ctx, kc, vc = pl.pallas_call(
        functools.partial(kernel, n_seq, block_rows),
        out_shape=(
            jax.ShapeDtypeStruct((rows, qw * tp), BF16),
            jax.ShapeDtypeStruct((frame, kw), BF16),
            jax.ShapeDtypeStruct((frame, kw), BF16),
        ),
        in_specs=[pl.BlockSpec(memory_space=pltpu.HBM)] * 8,
        out_specs=[pl.BlockSpec(memory_space=pl.ANY)] * 3,
        scratch_shapes=[
            pltpu.VMEM((1, width), F32),
            pltpu.VMEM((tp, rows), jnp.int32),
            pltpu.VMEM((1, home_blocks), jnp.int32),
            pltpu.VMEM((1, HD), F32),
            pltpu.VMEM((3, home_blocks, HD), F32),
            pltpu.VMEM((rows, width), BF16),
            pltpu.VMEM((tp, rows, width), BF16),
            pltpu.VMEM((nw, width, kw), BF16),
            pltpu.VMEM((nw, 2 * rows, kw), F32),
            pltpu.VMEM((nw, 2 * rows // HALVES, kw), F32),
            pltpu.VMEM((home, HD), F32),
            pltpu.VMEM((home, HD), F32),
            pltpu.VMEM((home, HD), F32),
            pltpu.VMEM((home, qw), BF16),
            pltpu.VMEM((DOC_MAX + home + spill, kw), BF16),
            pltpu.VMEM((DOC_MAX + home + spill, kw), BF16),
            pltpu.VMEM((2, 1, home_blocks), jnp.int32),
            pltpu.VMEM((tp, rows, qw), BF16),
            pltpu.VMEM((frame, kw), BF16),
            pltpu.VMEM((frame, kw), BF16),
            pltpu.SemaphoreType.DMA((6 + nw,)),
            pltpu.SemaphoreType.DMA((1,)),
            pltpu.SemaphoreType.DMA((1,)),
            pltpu.SemaphoreType.DMA((HALVES * COLS,)),
            pltpu.SemaphoreType.DMA((HALVES * COLS,)),
            pltpu.SemaphoreType.DMA((HALVES * COLS,)),
            pltpu.SemaphoreType.DMA((HALVES * COLS,)),
            pltpu.SemaphoreType.DMA((4 * HALVES,)),
            pltpu.SemaphoreType.DMA((4 * HALVES,)),
            pltpu.SemaphoreType.DMA((2 * HALVES,)),
            pltpu.SemaphoreType.DMA((2 * HALVES,)),
            pltpu.SemaphoreType.DMA((2,)),
            pltpu.SemaphoreType.DMA((2,)),
            pltpu.SemaphoreType.DMA((4 * HALVES,)),
            pltpu.SemaphoreType.DMA((4 * HALVES,)),
        ],
        compiler_params=pltpu.CompilerParams(
            collective_id=0, has_side_effects=True, vmem_limit_bytes=48 * 1024 * 1024),
    )(*(pltpu.with_memory_space_constraint(a, pltpu.HBM) for a in (
        hidden, norm_gain.reshape(1, width), w_query, w_key, w_value,
        doc_start.reshape(tp, rows),
        block_owner.reshape(1, home_blocks), freq,
    )))
    outs = (ctx, kc, vc)
    return pl.pallas_call(
        move,
        out_shape=tuple(jax.ShapeDtypeStruct(a.shape, a.dtype) for a in outs),
        in_specs=[pl.BlockSpec(memory_space=pl.ANY)] * 3,
        out_specs=[pl.BlockSpec(memory_space=pltpu.HBM)] * 3,
        scratch_shapes=[pltpu.SemaphoreType.DMA((3 * PIECES,))],
        compiler_params=pltpu.CompilerParams(vmem_limit_bytes=1024 * 1024),
    )(*outs)


def solution(mesh):
    return jax.shard_map(
        functools.partial(shards, mesh.shape["seq"], mesh.shape["tp"]),
        mesh=mesh,
        in_specs=(
            P(("seq", "tp"), None), P(), P(None, "tp"), P(None, "tp"), P(None, "tp"),
            P("seq"), P("seq"),
        ),
        out_specs=(P(("seq", "tp"), None), P("seq", "tp"), P("seq", "tp")),
        check_vma=False,
    )
```
